256 devices in a mesh: rows: 16 (over x, y), cols: 16 (over z, core).
Axes of the slice: x: 4, y: 4, z: 8, core: 2. Of those that a mesh axis runs over, the one named last changes fastest.
Arguments:
- power: float32 [2, 4, 2048, 2048], P(None, None, 'rows', 'cols'), may hold values from -6 to 6
- material: int32 [4, 2048, 2048], P(None, 'rows', 'cols'), may hold values from 0 to 7
- cond_table: float32 [4, 8], replicated, may hold values from 0.5 to 8
- tier_table: int32 [4], replicated, may hold values from 0 to 3
- coarse_slot: int32 [256], replicated, may hold values from 0 to 255, each once
- coarse_inverse: float32 [16, 16, 16], replicated, as said below
Outputs:
- solution: float32 [2, 4, 2048, 2048], P(None, None, 'rows', 'cols')
- residual: float32 [2, 4, 2048, 2048], P(None, None, 'rows', 'cols')
- precond: float32 [2, 4, 2048, 2048], P(None, None, 'rows', 'cols')
The draws below stay inside these ranges and needn't reach their ends.
Inputs may be any that keep to these rules, and one draw needn't show every extreme that they name: `coarse_slot`: each value once. `coarse_inverse`: symmetric within each owner.
All inputs are finite; a program needn't handle non-finite values.
Results may differ from the reference program's by a relative error of at most 0.0003.
Values sent between devices are 32-bit elements; how exact they have to be, the bound alone decides.
No kernel may reach another device: no remote copies, remote signals or barrier semaphores. Data moves between devices by JAX's collectives and lax.ppermute only.
A program may use at most 64 MiB of HBM per device.

```python
import math
import jax
import jax.numpy as jnp
from jax import lax

SUB = 128
VARIANTS = 2
TIERS = 4
MATS = 8
TABLES = 4
ITERS = 2
NX = 2048
NY = 2048
COARSE = 256
OWNERS = 16
OWN = 16


def draw_power(key, part):
    shape = (VARIANTS, TIERS, NX, NY)
    values = jnp.clip(jax.random.normal(key, shape, jnp.float32), -6.0, 6.0)
    return values


def draw_coarse_inverse(key, part):
    draw_key, spare_key = jax.random.split(jax.random.fold_in(key, 7))
    shape = (OWNERS, OWN, OWN)
    uniform_part = jax.random.uniform(draw_key, shape, jnp.float32, -1.0, 1.0)
    symmetric = 0.5 * (uniform_part + jnp.swapaxes(uniform_part, 1, 2)) * (12.0 / OWN)
    identity = jnp.eye(OWN, dtype=jnp.float32)[None, :, :]
    diagonal = jax.random.uniform(spare_key, shape, jnp.float32, 14.0, 30.0)
    return symmetric * (1.0 - identity) + diagonal * identity


def plant(array, key, least, top_value):
    longest = array.shape.index(max(array.shape))
    spots = []
    for shift in (0, 1):
        where = [jax.random.randint(jax.random.fold_in(key, axis), (), 0, length) for axis, length in enumerate(array.shape)]
        where[longest] = (where[longest] + shift) % array.shape[longest]
        spots.append(tuple(where))
    return array.at[spots[0]].set(least).at[spots[1]].set(top_value)


def setup_inputs(seed: int = 0) -> dict:
    seeds = jax.random.split(jax.random.key(seed), 7)
    return {
        "power": draw_power(jax.random.fold_in(seeds[6], 71), 0),
        "material": plant(jax.random.randint(seeds[1], (TIERS, NX, NY), 0, MATS), jax.random.fold_in(seeds[1], 1), 0, MATS - 1).astype(jnp.int32),
        "cond_table": jnp.clip(jnp.exp(jax.random.uniform(seeds[2], (TABLES, MATS), jnp.float32, math.log(0.5), math.log(8.0))), 0.5, 8.0),
        "tier_table": plant(jax.random.randint(seeds[3], (TIERS,), 0, TABLES), jax.random.fold_in(seeds[3], 1), 0, TABLES - 1).astype(jnp.int32),
        "coarse_slot": jax.random.permutation(seeds[4], COARSE).astype(jnp.int32),
        "coarse_inverse": draw_coarse_inverse(jax.random.fold_in(seeds[6], 71), 0),
    }


SHIFT_C = 0.5
VERT_C = 2.0
SINK_C = 0.05
HIGH = lax.Precision.HIGHEST

def sine_basis(length):
    counting = jnp.arange(1, length + 1).astype(jnp.float32)
    step_angle = math.pi / (length + 1)
    basis = math.sqrt(2.0 / (length + 1)) * jnp.sin(step_angle * counting[:, None] * counting[None, :])
    eigen_values = 2.0 - 2.0 * jnp.cos(step_angle * counting)
    return (basis, eigen_values)

def conductivity(material, cond_table, tier_table):
    tables = cond_table.shape[0]
    picker = (tier_table[:, None] == jnp.arange(tables, dtype=jnp.int32)[None, :]).astype(jnp.float32)
    tier_rows = jnp.dot(picker, cond_table, precision=HIGH)
    cond = jnp.zeros(material.shape, jnp.float32)
    for number in range(cond_table.shape[1]):
        cond = cond + jnp.where(material == number, tier_rows[:, number][:, None, None], 0.0)
    return (cond, lax.optimization_barrier(jnp.mean(tier_rows, axis=1)))

def coefficients(cond, padded):
    north = 0.5 * (cond + padded[:, :-2, 1:-1])
    south = 0.5 * (cond + padded[:, 2:, 1:-1])
    west = 0.5 * (cond + padded[:, 1:-1, :-2])
    east = 0.5 * (cond + padded[:, 1:-1, 2:])
    upward = VERT_C * 0.5 * (cond[:-1] + cond[1:])
    sink = jnp.concatenate([SINK_C * cond[:1], jnp.zeros_like(cond[1:])], 0)
    return (north, south, west, east, upward, sink)

def operate(temps, padded, coefs):
    north, south, west, east, upward, sink = coefs
    lateral = north * (temps - padded[:, :, :-2, 1:-1]) + south * (temps - padded[:, :, 2:, 1:-1])
    lateral = lateral + west * (temps - padded[:, :, 1:-1, :-2]) + east * (temps - padded[:, :, 1:-1, 2:])
    flux = upward * (temps[:, :-1] - temps[:, 1:])
    zeros_tier = jnp.zeros_like(temps[:, :1])
    vertical = jnp.concatenate([flux, zeros_tier], 1) - jnp.concatenate([zeros_tier, flux], 1)
    return lateral + vertical + sink * temps

def block_solve(temps, basis, denominator):
    shape = temps.shape
    length = basis.shape[0]
    blocks = temps.reshape(shape[0], shape[1], shape[2] // length, length, shape[3] // length, length)
    spectral = jnp.einsum('ia,vtxayb->vtxiyb', basis, blocks, precision=HIGH)
    spectral = jnp.einsum('vtxiyb,bj->vtxiyj', spectral, basis, precision=HIGH)
    spectral = spectral / denominator[None, :, None, :, None, :]
    result = jnp.einsum('ia,vtxayb->vtxiyb', basis, spectral, precision=HIGH)
    result = jnp.einsum('vtxiyb,bj->vtxiyj', result, basis, precision=HIGH)
    return result.reshape(shape)

def reference(power, material, cond_table, tier_table, coarse_slot, coarse_inverse):
    cond, mean_cond = conductivity(material, cond_table, tier_table)
    coefs = coefficients(cond, jnp.pad(cond, ((0, 0), (1, 1), (1, 1))))
    basis, eigen_values = sine_basis(SUB)
    denominator = mean_cond[:, None, None] * (eigen_values[:, None] + eigen_values[None, :] + SHIFT_C)
    half = SUB // 2
    scale = 1.0 / math.sqrt(SUB * SUB * TIERS)

    def apply_a(temps):
        return operate(temps, jnp.pad(temps, ((0, 0), (0, 0), (1, 1), (1, 1))), coefs)

    def precondition(resid):
        aligned = block_solve(resid, basis, denominator)
        moved = jnp.pad(resid, ((0, 0), (0, 0), (0, half), (0, half)))[:, :, half:, half:]
        offset = block_solve(moved, basis, denominator)
        offset = jnp.pad(offset, ((0, 0), (0, 0), (half, 0), (half, 0)))[:, :, :NX, :NY]
        sums = resid.reshape(VARIANTS, TIERS, NX // SUB, SUB, NY // SUB, SUB).sum(axis=(1, 3, 5)) * scale
        ordered = jnp.zeros((COARSE, VARIANTS), jnp.float32).at[coarse_slot].set(sums.reshape(VARIANTS, COARSE).T)
        solved = jnp.einsum('okj,ojv->okv', coarse_inverse, ordered.reshape(OWNERS, OWN, VARIANTS), precision=HIGH)
        picked = solved.reshape(COARSE, VARIANTS)[coarse_slot].T.reshape(VARIANTS, NX // SUB, NY // SUB)
        coarse = jnp.broadcast_to(picked[:, None, :, None, :, None], (VARIANTS, TIERS, NX // SUB, SUB, NY // SUB, SUB))
        return aligned + offset + coarse.reshape(resid.shape) * scale
    solution = jnp.zeros_like(power)
    residual = power
    precond = precondition(residual)
    direction = precond
    rz_now = lax.optimization_barrier(jnp.sum(residual * precond, axis=(1, 2, 3)))
    for number in range(ITERS):
        image = apply_a(direction)
        alpha = rz_now / lax.optimization_barrier(jnp.sum(direction * image, axis=(1, 2, 3)))
        solution = solution + alpha[:, None, None, None] * direction
        residual = residual - alpha[:, None, None, None] * image
        precond = precondition(residual)
        rz_next = lax.optimization_barrier(jnp.sum(residual * precond, axis=(1, 2, 3)))
        direction = precond + (rz_next / rz_now)[:, None, None, None] * direction
        rz_now = rz_next
    return (solution, residual, precond)
```

```python
import math

import numpy as np

import jax
import jax.numpy as jnp
from jax import lax
from jax.experimental import pallas as pl
from jax.experimental.pallas import tpu as pltpu
from jax.sharding import PartitionSpec as P

SUB = 128
HALF = 64
VARS = 2
TIERS = 4
SLABS = VARS * TIERS
SHIFT_C = 0.5
SINK_C = 0.05
HIGH = lax.Precision.HIGHEST
F32 = jnp.float32
BF16 = jnp.bfloat16
BOTH = ("rows", "cols")
EXT = 2 * SUB


def _split(mat):
    mat = np.asarray(mat, np.float32)
    top = mat.astype(BF16)
    low = (mat - top.astype(np.float32)).astype(BF16)
    return top, low


def _constants():
    n = np.arange(1, SUB + 1, dtype=np.float64)
    ang = math.pi / (SUB + 1)
    s = math.sqrt(2.0 / (SUB + 1)) * np.sin(ang * n[:, None] * n[None, :])
    ev = 2.0 - 2.0 * np.cos(ang * n)
    den = (ev[:, None] + ev[None, :] + SHIFT_C).astype(np.float32)
    pair = np.zeros((EXT, EXT))
    pair[:SUB, :SUB] = s
    pair[SUB:, SUB:] = s
    fwd = np.zeros((EXT, EXT))
    fwd[0:HALF, :SUB] = s[HALF:, :]
    fwd[SUB : SUB + HALF, :SUB] = s[:HALF, :]
    fwd[HALF:SUB, SUB:] = s[:HALF, :]
    fwd[SUB + HALF :, SUB:] = s[HALF:, :]
    inv = np.zeros((EXT, EXT))
    inv[:SUB, 0:HALF] = s[:, HALF:]
    inv[SUB:, HALF:SUB] = s[:, :HALF]
    inv_r = inv.copy()
    inv_r[:SUB, SUB] = s[:, HALF - 1]
    inv_r[SUB:, SUB + 1] = s[:, HALF]
    inv_c = inv.copy()
    inv_c[:SUB, SUB] = s[:, HALF - 1]
    inv_c[SUB:, EXT - 1] = s[:, HALF]
    return den, _split(pair), _split(fwd), _split(inv_r), _split(inv_c)


def _mm(x, top, low):
    xh = x.astype(BF16)
    xl = (x - xh.astype(F32)).astype(BF16)
    acc = jnp.dot(xh, top, preferred_element_type=F32)
    acc = acc + jnp.dot(xl, top, preferred_element_type=F32)
    return acc + jnp.dot(xh, low, preferred_element_type=F32)


def _iota(shape, dim):
    return lax.broadcasted_iota(jnp.int32, shape, dim)


def _tier_scalars(table, tiers):
    rows = []
    for t in range(TIERS):
        pick = tiers[t]
        rows.append([table[pick, m] for m in range(table.shape[1])])
    return rows


def _mean(row):
    total = row[0]
    for value in row[1:]:
        total = total + value
    return total * (1.0 / len(row))


def _flip2(x):
    return jnp.concatenate([x[:, :SUB].T, x[:, SUB:].T], axis=1)


def _aligned_tier(f0, f1, dinv, top, low):
    x = _mm(jnp.concatenate([f0, f1], axis=1), top, low)
    x = _mm(_flip2(x), top, low)
    x = x * jnp.concatenate([dinv, dinv], axis=1)
    x = _mm(x, top, low)
    x = _mm(_flip2(x), top, low)
    return x[:, :SUB], x[:, SUB:]


def _column_edges(get, count, col):
    lane = _iota((SUB, SUB), 1)
    acc = jnp.zeros((SUB, SUB), F32)
    for k in range(count):
        rolled = pltpu.roll(get(k), (k - col) % SUB, 1)
        acc = jnp.where(lane == k, rolled, acc)
    return acc.T[:16]


def _payload(values, ref):
    lane = _iota((1, SUB), 1)
    row = jnp.zeros((1, SUB), F32)
    for k, value in enumerate(values):
        row = jnp.where(lane == k, value, row)
    ref[...] = jnp.broadcast_to(row, ref.shape)


def _gathered(w_ref, gath_ref):
    return jnp.dot(w_ref[...], gath_ref[...], precision=HIGH, preferred_element_type=F32)


def _take(arr, row, lane):
    hit = (_iota(arr.shape, 0) == row) & (_iota(arr.shape, 1) == lane)
    return jnp.sum(jnp.where(hit, arr, 0.0))


def _ratio(arr, dist):
    return arr / pltpu.roll(arr, arr.shape[1] - dist, 1)


def _first(power, send_n, send_s, pay):
    sums = []
    for v in range(VARS):
        total = jnp.zeros((SUB, SUB), F32)
        for t in range(TIERS):
            x = power[v, t]
            send_n[v, t] = x[:HALF]
            send_s[v, t] = x[HALF:]
            total = total + x
        sums.append(jnp.sum(total))
    _payload(sums, pay)


def _prepare(n_rows, n_cols, own, power, material, table, tiers, slot_s, slot_v, inverse, den, top, low,
             al, cond, edge_n, edge_s, edge_w, edge_e, w_out):
    rows = _tier_scalars(table, tiers)
    for t in range(TIERS):
        mat = material[t]
        c = jnp.zeros((SUB, SUB), F32)
        for m, value in enumerate(rows[t]):
            c = jnp.where(mat == m, value, c)
        cond[t] = c
        dinv = 1.0 / (_mean(rows[t]) * den[...])
        a0, a1 = _aligned_tier(power[0, t], power[1, t], dinv, top[...], low[...])
        al[0, t] = a0
        al[1, t] = a1
    _edges(al, cond, edge_n, edge_s, edge_w, edge_e)
    total = n_rows * n_cols
    me = lax.axis_index("rows") * n_cols + lax.axis_index("cols")
    sub = _iota((8, total), 0)
    lane = _iota((8, total), 1)
    mine = jnp.full((8, total), -1, jnp.int32)
    for k, step in enumerate((0, -n_cols, n_cols, -1, 1)):
        g = jnp.minimum(jnp.maximum(me + step, 0), total - 1)
        mine = jnp.where(sub == k, slot_s[g], mine)
    picked = jnp.dot((mine == lane).astype(F32), inverse[...], precision=HIGH, preferred_element_type=F32)
    spread = (_iota((own, total), 1) % own == _iota((own, total), 0)).astype(F32)
    full = jnp.dot(picked, spread, precision=HIGH, preferred_element_type=F32)
    full = jnp.where((lane // own) == (mine // own), full, 0.0)
    place = (_iota((total, total), 0) == slot_v[...]).astype(F32)
    weights = jnp.dot(full, place, precision=HIGH, preferred_element_type=F32)
    weights = weights * (1.0 / (SUB * SUB * TIERS))
    w_out[...] = jnp.where(sub == 5, 1.0, weights)


def _edges(al, cond, edge_n, edge_s, edge_w, edge_e):
    for k in range(SLABS):
        edge_n[k : k + 1, :] = al[k // TIERS, k % TIERS, 0:1, :]
        edge_s[k : k + 1, :] = al[k // TIERS, k % TIERS, SUB - 1 : SUB, :]
    pad = jnp.zeros((16 - SLABS, SUB), F32)
    edge_n[SLABS:, :] = pad
    edge_s[SLABS:, :] = pad
    count = SLABS
    if cond is not None:
        count += TIERS
        for t in range(TIERS):
            edge_n[SLABS + t : SLABS + t + 1, :] = cond[t, 0:1, :]
            edge_s[SLABS + t : SLABS + t + 1, :] = cond[t, SUB - 1 : SUB, :]

    def get(k):
        return al[k // TIERS, k % TIERS] if k < SLABS else cond[k - SLABS]

    edge_w[...] = _column_edges(get, count, 0)
    edge_e[...] = _column_edges(get, count, SUB - 1)


def _align(with_edges, f, table, tiers, den, top, low, al, *edges):
    rows = _tier_scalars(table, tiers)
    for t in range(TIERS):
        dinv = 1.0 / (_mean(rows[t]) * den[...])
        a0, a1 = _aligned_tier(f[0, t], f[1, t], dinv, top[...], low[...])
        al[0, t] = a0
        al[1, t] = a1
    if with_edges:
        _edges(al, None, *edges)


def _pack(with_edges, f, got_n, got_s, *rest):
    if with_edges:
        edge_w, edge_e, send_w, send_e = rest
        send_w[TIERS * EXT :, :] = edge_w[...]
        send_e[TIERS * EXT :, :] = edge_e[...]
    else:
        send_w, send_e = rest
    for t in range(TIERS):
        at = t * EXT
        for part, size, start in ((f, SUB, 0), (got_n, HALF, SUB), (got_s, HALF, SUB + HALF)):
            x0 = part[0, t]
            x1 = part[1, t]
            left = _iota((size, SUB), 1) < HALF
            send_w[at + start : at + start + size, :] = jnp.where(left, x0, pltpu.roll(x1, HALF, 1))
            send_e[at + start : at + start + size, :] = jnp.where(left, pltpu.roll(x0, HALF, 1), x1)


def _offset_tier(t, halo, f, got_n, got_s, got_w, got_e, scale, fwd, inv_r, inv_c):
    wm = got_w[t * EXT : (t + 1) * EXT, :]
    em = got_e[t * EXT : (t + 1) * EXT, :]
    left = _iota((EXT, SUB), 1) < HALF
    side = (jnp.where(left, wm, pltpu.roll(em, HALF, 1)), jnp.where(left, pltpu.roll(wm, HALF, 1), em))
    stack = []
    for v in range(VARS):
        mid = jnp.concatenate([f[v, t], got_n[v, t], got_s[v, t]], axis=0)
        stack.append(jnp.concatenate([mid, side[v]], axis=1))
    x = _mm(jnp.concatenate(stack, axis=0), *fwd)
    x = jnp.concatenate([x[:EXT].T, x[EXT:].T], axis=0)
    x = _mm(x, *fwd)
    x = x * jnp.concatenate([scale, scale], axis=0)
    if halo:
        x = _mm(x, *inv_r)
        tall = [x[:EXT, :SUB].T, x[EXT:, :SUB].T, x[:EXT, SUB:].T[:8], x[EXT:, SUB:].T[:8]]
    else:
        x = _mm(x, inv_r[0][:, :SUB], inv_r[1][:, :SUB])
        tall = [x[:EXT].T, x[EXT:].T]
    x = jnp.concatenate(tall, axis=0)
    if not halo:
        x = _mm(x, inv_c[0][:, :SUB], inv_c[1][:, :SUB])
        return (x[:SUB], x[SUB:]), None, None
    x = _mm(x, *inv_c)
    tiles = (x[:SUB, :SUB], x[SUB:EXT, :SUB])
    sides = (x[:SUB, SUB:], x[SUB:EXT, SUB:])
    ends = (x[EXT : EXT + 8, :SUB], x[EXT + 8 :, :SUB])
    return tiles, ends, sides


def _scale(dinv):
    has_w = jnp.where(lax.axis_index("cols") > 0, 1.0, 0.0)
    has_n = jnp.where(lax.axis_index("rows") > 0, 1.0, 0.0)
    above = dinv * has_n
    return jnp.concatenate(
        [
            jnp.concatenate([above * has_w, dinv * has_w], axis=1),
            jnp.concatenate([above, dinv], axis=1),
        ],
        axis=0,
    )


def _solve(halo, f, got_n, got_s, got_w, got_e, al, near_n, near_s, table, tiers, den, fwd, inv_r, inv_c,
           y, y_rows, y_cols):
    rows = _tier_scalars(table, tiers)
    if halo:
        cols = _side_columns(got_w, got_e)
    for t in range(TIERS):
        dinv = 1.0 / (_mean(rows[t]) * den[...])
        tiles, ends, sides = _offset_tier(t, halo, f, got_n, got_s, got_w, got_e, _scale(dinv), fwd, inv_r, inv_c)
        for v in range(VARS):
            y[v, t] = tiles[v] + al[v, t]
            if halo:
                k = v * TIERS + t
                sub = _iota((8, SUB), 0)
                near = jnp.where(sub == 0, near_n[k : k + 1, :], near_s[k : k + 1, :])
                y_rows[v, t] = ends[v] + near
                y_cols[v, t] = sides[v] + _column_pair(cols, k)


def _side_columns(got_w, got_e):
    base = TIERS * EXT
    pad = jnp.zeros((SUB - 32, SUB), F32)
    return jnp.concatenate([got_w[base:, :], got_e[base:, :], pad], axis=0).T


def _column_pair(cols, k):
    lane = _iota((SUB, SUB), 1)
    west = pltpu.roll(cols, (SUB - k) % SUB, 1)
    east = pltpu.roll(cols, (SUB - 1 - 16 - k) % SUB, 1)
    return jnp.where(lane < HALF, west, east)


def _shifts(x, row_n, row_s, side):
    sub = _iota((SUB, SUB), 0)
    lane = _iota((SUB, SUB), 1)
    north = jnp.where(sub == 0, row_n, pltpu.roll(x, 1, 0))
    south = jnp.where(sub == SUB - 1, row_s, pltpu.roll(x, SUB - 1, 0))
    west = jnp.where(lane == 0, side, pltpu.roll(x, 1, 1))
    east = jnp.where(lane == SUB - 1, side, pltpu.roll(x, SUB - 1, 1))
    return north, south, west, east


def _inside(n_rows, n_cols):
    r = lax.axis_index("rows")
    c = lax.axis_index("cols")
    one = jnp.float32(1.0)
    zero = jnp.float32(0.0)
    return (
        jnp.where(r > 0, one, zero),
        jnp.where(r < n_rows - 1, one, zero),
        jnp.where(c > 0, one, zero),
        jnp.where(c < n_cols - 1, one, zero),
    )


def _operate(z, z_rows, z_cols, cond, c_rows, c_cols, out):
    for t in range(TIERS):
        c = cond[t]
        near = _shifts(c, c_rows[t, 0:1, :], c_rows[t, 1:2, :], c_cols[t])
        coefs = [0.5 * (c + n) for n in near]
        for v in range(VARS):
            u = z[v, t]
            around = _shifts(u, z_rows[v, t, 0:1, :], z_rows[v, t, 1:2, :], z_cols[v, t])
            acc = coefs[0] * (u - around[0])
            for k in range(1, 4):
                acc = acc + coefs[k] * (u - around[k])
            if t + 1 < TIERS:
                acc = acc + (c + cond[t + 1]) * (u - z[v, t + 1])
            if t > 0:
                acc = acc - (cond[t - 1] + c) * (z[v, t - 1] - u)
            if t == 0:
                acc = acc + SINK_C * c * u
            out[v, t] = acc


def _dot(a, b, v):
    total = jnp.zeros((SUB, SUB), F32)
    for t in range(TIERS):
        total = total + (a[v, t] * b[v, t] if b is not None else a[v, t])
    return jnp.sum(total)


def _begin(n_rows, n_cols, power, got_n, got_s, got_w, got_e, al, near_n, near_s, cond, w_ref, gath, table, tiers,
           den, fh, fl, rh, rl, ch, cl,
           y, y_rows, y_cols, s, send_n, send_s, pay, c_rows, c_cols, e_out, z, z_rows, z_cols):
    _solve(True, power, got_n, got_s, got_w, got_e, al, near_n, near_s, table, tiers, den,
           (fh[...], fl[...]), (rh[...], rl[...]), (ch[...], cl[...]), y, y_rows, y_cols)
    cols = _side_columns(got_w, got_e)
    sub = _iota((8, SUB), 0)
    for t in range(TIERS):
        k = SLABS + t
        c_rows[t] = jnp.where(sub == 0, near_n[k : k + 1, :], near_s[k : k + 1, :])
        c_cols[t] = _column_pair(cols, k)
    e = _gathered(w_ref, gath)
    e_out[...] = e
    inside = _inside(n_rows, n_cols)
    _add_coarse(e, 0, inside, y, y_rows, y_cols, z, z_rows, z_cols)
    _operate(z, z_rows, z_cols, cond, c_rows, c_cols, s)
    _send_rows(s, send_n, send_s)
    _payload(
        [_dot(power, z, v) for v in range(VARS)]
        + [_dot(z, s, v) for v in range(VARS)]
        + [_dot(s, None, v) for v in range(VARS)],
        pay,
    )


def _send_rows(s, send_n, send_s):
    for v in range(VARS):
        for t in range(TIERS):
            send_n[v, t] = s[v, t, :HALF]
            send_s[v, t] = s[v, t, HALF:]


def _add_coarse(e, base, inside, y, y_rows, y_cols, z, z_rows, z_cols):
    sub = _iota((8, SUB), 0)
    lane = _iota((SUB, SUB), 1)
    for v in range(VARS):
        own, north, south, west, east = [_take(e, k, base + v) for k in range(5)]
        for t in range(TIERS):
            z[v, t] = y[v, t] + own
            z_rows[v, t] = jnp.where(sub == 0, (y_rows[v, t] + north) * inside[0], (y_rows[v, t] + south) * inside[1])
            z_cols[v, t] = jnp.where(
                lane < HALF, (y_cols[v, t] + west) * inside[2], (y_cols[v, t] + east) * inside[3]
            )


def _second(f, got_n, got_s, got_w, got_e, al, near_n, near_s, table, tiers, den, fh, fl, rh, rl, ch, cl,
            y, y_rows, y_cols):
    _solve(True, f, got_n, got_s, got_w, got_e, al, near_n, near_s, table, tiers, den,
           (fh[...], fl[...]), (rh[...], rl[...]), (ch[...], cl[...]), y, y_rows, y_cols)


def _step(n_rows, n_cols, power, s0, y0, y0_rows, y0_cols, y1, y1_rows, y1_cols, cond, c_rows, c_cols, w_ref, e0,
          gath, r1, z1, w1, send_n, send_s, pay, keep, z_rows, z_cols):
    res = _gathered(w_ref, gath)
    quotient = _ratio(res, 2)
    alphas = [_take(quotient, 5, v) for v in range(VARS)]
    lane = _iota(res.shape, 1)
    moved = pltpu.roll(res, res.shape[1] - 4, 1)
    alpha_row = jnp.where(lane == 0, alphas[0], alphas[1])
    e1 = e0[...] - alpha_row * moved
    inside = _inside(n_rows, n_cols)
    sub = _iota((8, SUB), 0)
    wide = _iota((SUB, SUB), 1)
    for v in range(VARS):
        own, north, south, west, east = [_take(e1, k, v) for k in range(5)]
        a = alphas[v]
        for t in range(TIERS):
            r1[v, t] = power[v, t] - a * s0[v, t]
            z1[v, t] = (y0[v, t] - a * y1[v, t]) + own
            ends = y0_rows[v, t] - a * y1_rows[v, t]
            z_rows[v, t] = jnp.where(sub == 0, (ends + north) * inside[0], (ends + south) * inside[1])
            side = y0_cols[v, t] - a * y1_cols[v, t]
            z_cols[v, t] = jnp.where(wide < HALF, (side + west) * inside[2], (side + east) * inside[3])
    _operate(z1, z_rows, z_cols, cond, c_rows, c_cols, w1)
    _send_rows(w1, send_n, send_s)
    _payload(
        [_dot(r1, z1, v) for v in range(VARS)]
        + [_dot(z1, w1, v) for v in range(VARS)]
        + [_dot(z1, s0, v) for v in range(VARS)]
        + [_dot(w1, None, v) for v in range(VARS)],
        pay,
    )
    row = jnp.zeros((8, SUB), F32)
    kl = _iota((8, SUB), 1)
    for v in range(VARS):
        for k, value in enumerate(
            (_take(res, 5, v), _take(res, 5, 2 + v), alphas[v], _take(e0[...], 0, v), _take(res, 0, 4 + v))
        ):
            row = jnp.where(kl == 2 * k + v, value, row)
    keep[...] = row


def _third(f, got_n, got_s, got_w, got_e, al, table, tiers, den, fh, fl, rh, rl, ch, cl, y):
    _solve(False, f, got_n, got_s, got_w, got_e, al, None, None, table, tiers, den,
           (fh[...], fl[...]), (rh[...], rl[...]), (ch[...], cl[...]), y, None, None)


def _finish(s0, y0, y1, r1, z1, w1, y2, w_ref, keep, gath, x_out, r_out, z_out):
    res = _gathered(w_ref, gath)
    k = keep[...]
    for v in range(VARS):
        def wide(value):
            return jnp.full((8, SUB), 1.0, F32) * value

        rz0, d0, a0, e0, cs = [_take(k, 0, 2 * j + v) for j in range(5)]
        rz1, d1, zs = [_take(res, 5, 2 * j + v) for j in range(3)]
        cw = _take(res, 0, 6 + v)
        beta_w = wide(rz1) / wide(rz0)
        den = wide(d1) + 2.0 * beta_w * wide(zs) + beta_w * beta_w * wide(d0)
        alpha = _take(wide(rz1) / den, 0, 0)
        beta = _take(beta_w, 0, 0)
        change = -alpha * (cw + beta * cs)
        for t in range(TIERS):
            z = z1[v, t]
            x_out[v, t] = a0 * (y0[v, t] + e0) + alpha * (z + beta * (y0[v, t] + e0))
            r_out[v, t] = r1[v, t] - alpha * (w1[v, t] + beta * s0[v, t])
            z_out[v, t] = (z - alpha * (y2[v, t] + beta * y1[v, t])) + change


def _call(body, outs, args, smem=(), scratch=()):
    specs = [
        pl.BlockSpec(memory_space=pltpu.SMEM if i in smem else pltpu.VMEM) for i in range(len(args))
    ]
    return pl.pallas_call(
        body,
        out_shape=[jax.ShapeDtypeStruct(s, F32) for s in outs],
        in_specs=specs,
        out_specs=[pl.BlockSpec(memory_space=pltpu.VMEM) for _ in outs],
        scratch_shapes=[pltpu.VMEM(s, F32) for s in scratch],
        compiler_params=pltpu.CompilerParams(vmem_limit_bytes=48 << 20),
    )(*args)


FIELD = (VARS, TIERS, SUB, SUB)
MARGIN = (VARS, TIERS, HALF, SUB)
ENDS = (VARS, TIERS, 8, SUB)
EDGE = (16, SUB)


def _exchange(first, second, axis):
    count = lax.axis_size(axis)
    before = lax.ppermute(second, axis, [(i, i + 1) for i in range(count - 1)])
    after = lax.ppermute(first, axis, [(i + 1, i) for i in range(count - 1)])
    return before, after


def _everywhere(pay):
    return lax.all_to_all(pay, BOTH, 0, 0, tiled=True)


def shards(power, material, cond_table, tier_table, coarse_slot, coarse_inverse):
    n_rows = lax.axis_size("rows")
    n_cols = lax.axis_size("cols")
    total = n_rows * n_cols
    own = coarse_inverse.shape[1]
    den, pair, fwd, inv_r, inv_c = _constants()
    den = jnp.asarray(den)
    pair, fwd, inv_r, inv_c = [tuple(jnp.asarray(m) for m in two) for two in (pair, fwd, inv_r, inv_c)]
    mats = (den, *fwd, *inv_r, *inv_c)
    pay_shape = (total, SUB)
    message = (TIERS * EXT + 16, SUB)
    bare = (TIERS * EXT, SUB)

    send_n, send_s, pay = _call(_first, [MARGIN, MARGIN, pay_shape], [power])
    gath_a = _everywhere(pay)
    got_n, got_s = _exchange(send_n, send_s, "rows")
    al, cond, edge_n, edge_s, edge_w, edge_e, weights = _call(
        lambda *refs: _prepare(n_rows, n_cols, own, *refs),
        [FIELD, (TIERS, SUB, SUB), EDGE, EDGE, EDGE, EDGE, (8, total)],
        [power, material, cond_table, tier_table, coarse_slot, coarse_slot.reshape(1, total),
         coarse_inverse.reshape(total, own), den, *pair],
        smem=(2, 3, 4),
    )
    near_n, near_s = _exchange(edge_n, edge_s, "rows")
    send_w, send_e = _call(
        lambda *refs: _pack(True, *refs), [message, message], [power, got_n, got_s, edge_w, edge_e]
    )
    got_w, got_e = _exchange(send_w, send_e, "cols")
    y0, y0_rows, y0_cols, s0, send_n, send_s, pay, c_rows, c_cols, e0 = _call(
        lambda *refs: _begin(n_rows, n_cols, *refs),
        [FIELD, ENDS, FIELD, FIELD, MARGIN, MARGIN, pay_shape, (TIERS, 8, SUB), (TIERS, SUB, SUB), (8, SUB)],
        [power, got_n, got_s, got_w, got_e, al, near_n, near_s, cond, weights, gath_a, cond_table, tier_table, *mats],
        smem=(11, 12),
        scratch=(FIELD, ENDS, FIELD),
    )

    gath_b = _everywhere(pay)
    got_n, got_s = _exchange(send_n, send_s, "rows")
    al, edge_n, edge_s, edge_w, edge_e = _call(
        lambda *refs: _align(True, *refs),
        [FIELD, EDGE, EDGE, EDGE, EDGE],
        [s0, cond_table, tier_table, den, *pair],
        smem=(1, 2),
    )
    near_n, near_s = _exchange(edge_n, edge_s, "rows")
    send_w, send_e = _call(
        lambda *refs: _pack(True, *refs), [message, message], [s0, got_n, got_s, edge_w, edge_e]
    )
    got_w, got_e = _exchange(send_w, send_e, "cols")
    y1, y1_rows, y1_cols = _call(
        _second,
        [FIELD, ENDS, FIELD],
        [s0, got_n, got_s, got_w, got_e, al, near_n, near_s, cond_table, tier_table, *mats],
        smem=(8, 9),
    )
    r1, z1, w1, send_n, send_s, pay, keep = _call(
        lambda *refs: _step(n_rows, n_cols, *refs),
        [FIELD, FIELD, FIELD, MARGIN, MARGIN, pay_shape, (8, SUB)],
        [power, s0, y0, y0_rows, y0_cols, y1, y1_rows, y1_cols, cond, c_rows, c_cols, weights, e0, gath_b],
        scratch=(ENDS, FIELD),
    )

    gath_c = _everywhere(pay)
    got_n, got_s = _exchange(send_n, send_s, "rows")
    (al,) = _call(
        lambda *refs: _align(False, *refs), [FIELD], [w1, cond_table, tier_table, den, *pair], smem=(1, 2)
    )
    send_w, send_e = _call(lambda *refs: _pack(False, *refs), [bare, bare], [w1, got_n, got_s])
    got_w, got_e = _exchange(send_w, send_e, "cols")
    (y2,) = _call(
        _third, [FIELD], [w1, got_n, got_s, got_w, got_e, al, cond_table, tier_table, *mats], smem=(6, 7)
    )
    return tuple(
        _call(_finish, [FIELD, FIELD, FIELD], [s0, y0, y1, r1, z1, w1, y2, weights, keep, gath_c])
    )


def solution(mesh):
    in_specs = (P(None, None, "rows", "cols"), P(None, "rows", "cols"), P(), P(), P(), P())
    out_specs = (P(None, None, "rows", "cols"),) * 3
    return jax.shard_map(shards, mesh=mesh, in_specs=in_specs, out_specs=out_specs, check_vma=False)
```

```python
import math

import numpy as np

import jax
import jax.numpy as jnp
from jax import lax
from jax.experimental import pallas as pl
from jax.experimental.pallas import tpu as pltpu
from jax.sharding import PartitionSpec as P

SUB = 128
HALF = 64
VARS = 2
TIERS = 4
SLABS = VARS * TIERS
SHIFT_C = 0.5
SINK_C = 0.05
HIGH = lax.Precision.HIGHEST
F32 = jnp.float32
BF16 = jnp.bfloat16
BOTH = ("rows", "cols")
EXT = 2 * SUB


MARG = SLABS * HALF


def _doubled(mat):
    mat = np.asarray(mat, np.float32)
    top = mat.astype(BF16)
    low = (mat - top.astype(np.float32)).astype(BF16)
    return np.concatenate([np.concatenate([top, low], 1)] * 2, 0)


def _constants():
    n = np.arange(1, SUB + 1, dtype=np.float64)
    ang = math.pi / (SUB + 1)
    s = math.sqrt(2.0 / (SUB + 1)) * np.sin(ang * n[:, None] * n[None, :])
    ev = 2.0 - 2.0 * np.cos(ang * n)
    den = (ev[:, None] + ev[None, :] + SHIFT_C).astype(np.float32)
    turned = np.roll(s, HALF, axis=0)
    return [jnp.asarray(a) for a in (den, _doubled(s), _doubled(turned), _doubled(turned.T))]


def _mm(x, mat):
    xh = x.astype(BF16)
    xl = (x - xh.astype(F32)).astype(BF16)
    both = jnp.dot(jnp.concatenate([xh, xl], axis=1), mat, preferred_element_type=F32)
    return both[:, :SUB] + both[:, SUB:]


def _iota(shape, dim):
    return lax.broadcasted_iota(jnp.int32, shape, dim)


def _left(rows):
    return _iota((rows, SUB), 1) < HALF


def _tier_scalars(table, tiers):
    rows = []
    for t in range(TIERS):
        pick = tiers[t]
        rows.append([table[pick, m] for m in range(table.shape[1])])
    return rows


def _mean(row):
    total = row[0]
    for value in row[1:]:
        total = total + value
    return total * (1.0 / len(row))


def _parts(x, size=SUB):
    return [x[i : i + size] for i in range(0, x.shape[0], size)]


def _interleave(works):
    live = []
    works = list(works)
    while works or live:
        if works:
            live.append(works.pop(0))
        for work in list(live):
            try:
                next(work)
            except StopIteration:
                live.remove(work)


def _aligned_tier(t, f, dinv, mat, al):
    x = _mm(jnp.concatenate([f[v, t] for v in range(VARS)], axis=0), mat)
    yield
    x = _mm(jnp.concatenate([p.T for p in _parts(x)], axis=0), mat)
    yield
    x = _mm(x * jnp.concatenate([dinv] * VARS, axis=0), mat)
    yield
    x = _mm(jnp.concatenate([p.T for p in _parts(x)], axis=0), mat)
    yield
    for v, p in enumerate(_parts(x)):
        al[v, t] = p


def _align_all(f, rows, den, mat, al):
    _interleave(_aligned_tier(t, f, 1.0 / (_mean(rows[t]) * den[...]), mat[...], al) for t in range(TIERS))


def _column_edges(get, count, col):
    lane = _iota((SUB, SUB), 1)
    acc = jnp.zeros((SUB, SUB), F32)
    for k in range(count):
        rolled = pltpu.roll(get(k), (k - col) % SUB, 1)
        acc = jnp.where(lane == k, rolled, acc)
    return acc.T[:16]


def _row(values, ref):
    lane = _iota(ref.shape, 1)
    row = jnp.zeros(ref.shape, F32)
    for k, value in enumerate(values):
        row = jnp.where(lane == k, value, row)
    ref[...] = row


def _gathered(w_ref, gath_ref):
    return jnp.dot(w_ref[...], gath_ref[...], precision=HIGH, preferred_element_type=F32)


def _take(arr, row, lane):
    hit = (_iota(arr.shape, 0) == row) & (_iota(arr.shape, 1) == lane)
    return jnp.sum(jnp.where(hit, arr, 0.0))


def _ratio(arr, dist):
    return arr / pltpu.roll(arr, arr.shape[1] - dist, 1)


def _send_rows(s, send_n, send_s):
    for v in range(VARS):
        for t in range(TIERS):
            at = (v * TIERS + t) * HALF
            send_n[at : at + HALF, :] = s[v, t, :HALF]
            send_s[at : at + HALF, :] = s[v, t, HALF:]


def _edges(al, cond, send_n, send_s, edge_w, edge_e):
    count = SLABS if cond is None else SLABS + TIERS

    def get(k):
        return al[k // TIERS, k % TIERS] if k < SLABS else cond[k - SLABS]

    zero = jnp.zeros((16, SUB), F32)
    send_n[MARG:, :] = zero
    send_s[MARG:, :] = zero
    for k in range(count):
        x = get(k)
        send_n[MARG + k : MARG + k + 1, :] = x[0:1]
        send_s[MARG + k : MARG + k + 1, :] = x[SUB - 1 : SUB]
    edge_w[...] = _column_edges(get, count, 0)
    edge_e[...] = _column_edges(get, count, SUB - 1)


def _prepare(power, material, table, tiers, den, mat, al, cond, send_n, send_s, edge_w, edge_e, row):
    rows = _tier_scalars(table, tiers)
    for t in range(TIERS):
        ids = material[t]
        c = jnp.zeros((SUB, SUB), F32)
        for m, value in enumerate(rows[t]):
            c = jnp.where(ids == m, value, c)
        cond[t] = c
    _send_rows(power, send_n, send_s)
    _row([_dot(power, None, v) for v in range(VARS)], row)
    _align_all(power, rows, den, mat, al)
    _edges(al, cond, send_n, send_s, edge_w, edge_e)


def _weigh(n_rows, n_cols, own, slot_s, slot_v, inverse, w_out):
    total = n_rows * n_cols
    me = lax.axis_index("rows") * n_cols + lax.axis_index("cols")
    sub = _iota((8, total), 0)
    lane = _iota((8, total), 1)
    mine = jnp.full((8, total), -1, jnp.int32)
    for k, step in enumerate((0, -n_cols, n_cols, -1, 1)):
        g = jnp.minimum(jnp.maximum(me + step, 0), total - 1)
        mine = jnp.where(sub == k, slot_s[g], mine)
    picked = jnp.dot((mine == lane).astype(F32), inverse[...], precision=HIGH, preferred_element_type=F32)
    spread = (_iota((own, total), 1) % own == _iota((own, total), 0)).astype(F32)
    full = jnp.dot(picked, spread, precision=HIGH, preferred_element_type=F32)
    full = jnp.where((lane // own) == (mine // own), full, 0.0)
    place = (_iota((total, total), 0) == slot_v[...]).astype(F32)
    weights = jnp.dot(full, place, precision=HIGH, preferred_element_type=F32)
    weights = weights * (1.0 / (SUB * SUB * TIERS))
    w_out[...] = jnp.where(sub == 5, 1.0, weights)


def _ext_rows(f, got_n, got_s, v, t):
    at = (v * TIERS + t) * HALF
    x = f[v, t]
    return [x[:HALF], got_n[at : at + HALF, :], got_s[at : at + HALF, :], x[HALF:]]


def _pack(f, got_n, got_s, row, *rest):
    if len(rest) == 5:
        edge_w, edge_e, send_w, send_e, pay = rest
        send_w[TIERS * EXT :, :] = edge_w[...]
        send_e[TIERS * EXT :, :] = edge_e[...]
    else:
        send_w, send_e, pay = rest
    pay[...] = jnp.broadcast_to(row[0:1, :], pay.shape)
    left = _left(HALF)
    for t in range(TIERS):
        for part in range(4):
            at = t * EXT + part * HALF
            x0 = _ext_rows(f, got_n, got_s, 0, t)[part]
            x1 = _ext_rows(f, got_n, got_s, 1, t)[part]
            send_w[at : at + HALF, :] = jnp.where(left, x0, pltpu.roll(x1, HALF, 1))
            send_e[at : at + HALF, :] = jnp.where(left, pltpu.roll(x1, HALF, 1), x0)


def _offset_tier(t, halo, f, got_n, got_s, got_w, got_e, dinv, masks, fwd, inv, use):
    wm = got_w[t * EXT : (t + 1) * EXT, :]
    em = got_e[t * EXT : (t + 1) * EXT, :]
    left = _left(EXT)
    stack = []
    for v in range(VARS):
        mid = jnp.concatenate(_ext_rows(f, got_n, got_s, v, t), axis=0)
        before = wm if v == 0 else pltpu.roll(wm, HALF, 1)
        after = em if v == 0 else pltpu.roll(em, HALF, 1)
        stack += [jnp.where(left, mid, before), jnp.where(left, after, mid)]
    x = _mm(jnp.concatenate(stack, axis=0), fwd)
    yield
    stack = []
    for p in _parts(x, EXT):
        stack += [p[:SUB].T, p[SUB:].T]
    x = _mm(jnp.concatenate(stack, axis=0), fwd)
    yield
    has_n, has_w = masks
    quarter = [dinv * (has_w * has_n), dinv * has_w, dinv * has_n, dinv]
    x = _mm(x * jnp.concatenate(quarter * VARS, axis=0), inv)
    yield
    left = _left(SUB)
    stack = []
    parts = _parts(x)
    for i in range(0, len(parts), 2):
        stack.append(jnp.where(left, parts[i], parts[i + 1]).T)
        if halo:
            other = jnp.where(left, parts[i + 1], parts[i]).T
            stack += [other[:8], other[SUB - 8 :]]
    x = _mm(jnp.concatenate(stack, axis=0), inv)
    yield
    parts = _parts(x, SUB + 16 if halo else SUB)
    for v in range(VARS):
        a, b = parts[2 * v : 2 * v + 2]
        tile = jnp.where(left, a[:SUB], b[:SUB])
        if halo:
            use(v, t, tile, jnp.where(_left(16), a[SUB:], b[SUB:]), jnp.where(left, b[:SUB], a[:SUB]))
        else:
            use(v, t, tile, None, None)


def _masks():
    return (jnp.where(lax.axis_index("rows") > 0, 1.0, 0.0), jnp.where(lax.axis_index("cols") > 0, 1.0, 0.0))


def _solve(f, got_n, got_s, got_w, got_e, al, rows, den, fwd, inv, y, y_rows, y_cols):
    cols = _side_columns(got_w, got_e)
    low = _iota((16, SUB), 0) < 8

    def use(v, t, tile, ends, side):
        k = v * TIERS + t
        y[v, t] = tile + al[v, t]
        at = MARG + k
        y_rows[v, t] = ends + jnp.where(low, got_s[at : at + 1, :], got_n[at : at + 1, :])
        y_cols[v, t] = side + _column_pair(cols, k)

    _interleave(
        _offset_tier(t, True, f, got_n, got_s, got_w, got_e, 1.0 / (_mean(rows[t]) * den[...]), _masks(),
                     fwd[...], inv[...], use)
        for t in range(TIERS)
    )
    return cols


def _side_columns(got_w, got_e):
    base = TIERS * EXT
    pad = jnp.zeros((SUB - 32, SUB), F32)
    return jnp.concatenate([got_w[base:, :], got_e[base:, :], pad], axis=0).T


def _column_pair(cols, k):
    west = pltpu.roll(cols, SUB - 1 - k, 1)
    east = pltpu.roll(cols, SUB - 16 - k, 1)
    return jnp.where(_left(SUB), east, west)


def _shifts(x, ends, side):
    sub = _iota((SUB, SUB), 0)
    lane = _iota((SUB, SUB), 1)
    north = jnp.where(sub == 0, ends[15:16, :], pltpu.roll(x, 1, 0))
    south = jnp.where(sub == SUB - 1, ends[0:1, :], pltpu.roll(x, SUB - 1, 0))
    west = pltpu.roll(jnp.where(lane == SUB - 1, side, x), 1, 1)
    east = pltpu.roll(jnp.where(lane == 0, side, x), SUB - 1, 1)
    return north, south, west, east


def _inside(n_rows, n_cols):
    r = lax.axis_index("rows")
    c = lax.axis_index("cols")
    one = jnp.float32(1.0)
    zero = jnp.float32(0.0)
    return (
        jnp.where(r > 0, one, zero),
        jnp.where(r < n_rows - 1, one, zero),
        jnp.where(c > 0, one, zero),
        jnp.where(c < n_cols - 1, one, zero),
    )


def _operate(z, z_rows, z_cols, cond, c_rows, c_cols, out):
    for t in range(TIERS):
        c = cond[t]
        coefs = [0.5 * (c + n) for n in _shifts(c, c_rows[t], c_cols[t])]
        for v in range(VARS):
            u = z[v, t]
            around = _shifts(u, z_rows[v, t], z_cols[v, t])
            acc = coefs[0] * (u - around[0])
            for k in range(1, 4):
                acc = acc + coefs[k] * (u - around[k])
            if t + 1 < TIERS:
                acc = acc + (c + cond[t + 1]) * (u - z[v, t + 1])
            if t > 0:
                acc = acc - (cond[t - 1] + c) * (z[v, t - 1] - u)
            if t == 0:
                acc = acc + SINK_C * c * u
            out[v, t] = acc


def _dot(a, b, v):
    total = jnp.zeros((SUB, SUB), F32)
    for t in range(TIERS):
        total = total + (a[v, t] * b[v, t] if b is not None else a[v, t])
    return jnp.sum(total)


def _around(y_rows, y_cols, e, base, v, inside):
    north, south, west, east = [_take(e, k, base + v) for k in range(1, 5)]
    low = _iota((16, SUB), 0) < 8
    left = _left(SUB)
    return (
        jnp.where(low, (y_rows + south) * inside[1], (y_rows + north) * inside[0]),
        jnp.where(left, (y_cols + east) * inside[3], (y_cols + west) * inside[2]),
    )


def _begin(n_rows, n_cols, power, got_n, got_s, got_w, got_e, al, cond, w_ref, gath, table, tiers, den, mat, fwd, inv,
           y, y_rows, y_cols, s, al_s, send_n, send_s, edge_w, edge_e, row, c_rows, c_cols, e_out, z, z_rows, z_cols):
    rows = _tier_scalars(table, tiers)
    cols = _solve(power, got_n, got_s, got_w, got_e, al, rows, den, fwd, inv, y, y_rows, y_cols)
    low = _iota((16, SUB), 0) < 8
    for t in range(TIERS):
        at = MARG + SLABS + t
        c_rows[t] = jnp.where(low, got_s[at : at + 1, :], got_n[at : at + 1, :])
        c_cols[t] = _column_pair(cols, SLABS + t)
    e = _gathered(w_ref, gath)
    e_out[...] = e
    inside = _inside(n_rows, n_cols)
    for v in range(VARS):
        own = _take(e, 0, v)
        for t in range(TIERS):
            z[v, t] = y[v, t] + own
            z_rows[v, t], z_cols[v, t] = _around(y_rows[v, t], y_cols[v, t], e, 0, v, inside)
    _operate(z, z_rows, z_cols, cond, c_rows, c_cols, s)
    _send_rows(s, send_n, send_s)
    _align_all(s, rows, den, mat, al_s)
    _edges(al_s, None, send_n, send_s, edge_w, edge_e)
    _row(
        [_dot(power, z, v) for v in range(VARS)]
        + [_dot(z, s, v) for v in range(VARS)]
        + [_dot(s, None, v) for v in range(VARS)],
        row,
    )


def _step(n_rows, n_cols, power, s0, got_n, got_s, got_w, got_e, al, y0, y0_rows, y0_cols, cond, c_rows, c_cols,
          w_ref, e0, gath, table, tiers, den, fwd, inv,
          y1, r1, z1, w1, send_n, send_s, row, keep, y1_rows, y1_cols, z_rows, z_cols):
    rows = _tier_scalars(table, tiers)
    _solve(s0, got_n, got_s, got_w, got_e, al, rows, den, fwd, inv, y1, y1_rows, y1_cols)
    res = _gathered(w_ref, gath)
    quotient = _ratio(res, 2)
    alphas = [_take(quotient, 5, v) for v in range(VARS)]
    lane = _iota(res.shape, 1)
    moved = pltpu.roll(res, res.shape[1] - 4, 1)
    e1 = e0[...] - jnp.where(lane == 0, alphas[0], alphas[1]) * moved
    inside = _inside(n_rows, n_cols)
    for v in range(VARS):
        own = _take(e1, 0, v)
        a = alphas[v]
        for t in range(TIERS):
            r1[v, t] = power[v, t] - a * s0[v, t]
            z1[v, t] = (y0[v, t] - a * y1[v, t]) + own
            z_rows[v, t], z_cols[v, t] = _around(
                y0_rows[v, t] - a * y1_rows[v, t], y0_cols[v, t] - a * y1_cols[v, t], e1, 0, v, inside
            )
    _operate(z1, z_rows, z_cols, cond, c_rows, c_cols, w1)
    _send_rows(w1, send_n, send_s)
    _row(
        [_dot(r1, z1, v) for v in range(VARS)]
        + [_dot(z1, w1, v) for v in range(VARS)]
        + [_dot(z1, s0, v) for v in range(VARS)]
        + [_dot(w1, None, v) for v in range(VARS)],
        row,
    )
    kept = []
    for values in ((res, 5, 0), (res, 5, 2), None, (e0[...], 0, 0), (res, 0, 4)):
        kept += alphas if values is None else [_take(values[0], values[1], values[2] + v) for v in range(VARS)]
    _row(kept, keep)


def _align_last(f, table, tiers, den, mat, al):
    _align_all(f, _tier_scalars(table, tiers), den, mat, al)


def _finish(s0, y0, y1, r1, z1, w1, got_n, got_s, got_w, got_e, al, w_ref, keep, gath, table, tiers, den, fwd, inv,
            x_out, r_out, z_out):
    rows = _tier_scalars(table, tiers)
    res = _gathered(w_ref, gath)
    k = keep[...]
    values = []
    for v in range(VARS):
        def wide(value):
            return jnp.full((8, SUB), 1.0, F32) * value

        rz0, d0, a0, e0, cs = [_take(k, 0, 2 * j + v) for j in range(5)]
        rz1, d1, zs = [_take(res, 5, 2 * j + v) for j in range(3)]
        cw = _take(res, 0, 6 + v)
        beta_w = wide(rz1) / wide(rz0)
        below = wide(d1) + 2.0 * beta_w * wide(zs) + beta_w * beta_w * wide(d0)
        alpha = _take(wide(rz1) / below, 0, 0)
        beta = _take(beta_w, 0, 0)
        values.append((a0, e0, alpha, beta, -alpha * (cw + beta * cs)))

    def use(v, t, tile, ends, side):
        a0, e0, alpha, beta, change = values[v]
        z = z1[v, t]
        first = y0[v, t] + e0
        x_out[v, t] = a0 * first + alpha * (z + beta * first)
        r_out[v, t] = r1[v, t] - alpha * (w1[v, t] + beta * s0[v, t])
        z_out[v, t] = (z - alpha * ((tile + al[v, t]) + beta * y1[v, t])) + change

    _interleave(
        _offset_tier(t, False, w1, got_n, got_s, got_w, got_e, 1.0 / (_mean(rows[t]) * den[...]), _masks(),
                     fwd[...], inv[...], use)
        for t in range(TIERS)
    )


def _call(body, outs, args, smem=(), scratch=()):
    specs = [
        pl.BlockSpec(memory_space=pltpu.SMEM if i in smem else pltpu.VMEM) for i in range(len(args))
    ]
    return pl.pallas_call(
        body,
        out_shape=[jax.ShapeDtypeStruct(s, F32) for s in outs],
        in_specs=specs,
        out_specs=[pl.BlockSpec(memory_space=pltpu.VMEM) for _ in outs],
        scratch_shapes=[pltpu.VMEM(s, F32) for s in scratch],
        compiler_params=pltpu.CompilerParams(vmem_limit_bytes=VMEM_LIMIT),
    )(*args)


VMEM_LIMIT = 16 << 20
FIELD = (VARS, TIERS, SUB, SUB)
ENDS = (VARS, TIERS, 16, SUB)
EDGE = (16, SUB)
ROW = (8, SUB)
TIER_FIELD = (TIERS, SUB, SUB)
MARGIN = (MARG + 16, SUB)
BARE_MARGIN = (MARG, SUB)
SIDE = (TIERS * EXT + 16, SUB)
BARE_SIDE = (TIERS * EXT, SUB)


def _exchange(first, second, axis):
    count = lax.axis_size(axis)
    before = lax.ppermute(second, axis, [(i, i + 1) for i in range(count - 1)])
    after = lax.ppermute(first, axis, [(i + 1, i) for i in range(count - 1)])
    return before, after


def _everywhere(pay):
    return lax.all_to_all(pay, BOTH, 0, 0, tiled=True)


def shards(power, material, cond_table, tier_table, coarse_slot, coarse_inverse):
    n_rows = lax.axis_size("rows")
    n_cols = lax.axis_size("cols")
    total = n_rows * n_cols
    own = coarse_inverse.shape[1]
    den, mat, fwd, inv = _constants()
    pay_shape = (total, SUB)

    (weights,) = _call(
        lambda *refs: _weigh(n_rows, n_cols, own, *refs),
        [(8, total)],
        [coarse_slot, coarse_slot.reshape(1, total), coarse_inverse.reshape(total, own)],
        smem=(0,),
    )
    al, cond, send_n, send_s, edge_w, edge_e, row = _call(
        _prepare,
        [FIELD, TIER_FIELD, MARGIN, MARGIN, EDGE, EDGE, ROW],
        [power, material, cond_table, tier_table, den, mat],
        smem=(2, 3),
    )
    got_n, got_s = _exchange(send_n, send_s, "rows")
    send_w, send_e, pay = _call(_pack, [SIDE, SIDE, pay_shape], [power, got_n, got_s, row, edge_w, edge_e])
    got_w, got_e = _exchange(send_w, send_e, "cols")
    gath = _everywhere(pay)
    y0, y0_rows, y0_cols, s0, al, send_n, send_s, edge_w, edge_e, row, c_rows, c_cols, e0 = _call(
        lambda *refs: _begin(n_rows, n_cols, *refs),
        [FIELD, ENDS, FIELD, FIELD, FIELD, MARGIN, MARGIN, EDGE, EDGE, ROW, (TIERS, 16, SUB), TIER_FIELD, ROW],
        [power, got_n, got_s, got_w, got_e, al, cond, weights, gath, cond_table, tier_table, den, mat, fwd, inv],
        smem=(9, 10),
        scratch=(FIELD, ENDS, FIELD),
    )

    got_n, got_s = _exchange(send_n, send_s, "rows")
    send_w, send_e, pay = _call(_pack, [SIDE, SIDE, pay_shape], [s0, got_n, got_s, row, edge_w, edge_e])
    got_w, got_e = _exchange(send_w, send_e, "cols")
    gath = _everywhere(pay)
    y1, r1, z1, w1, send_n, send_s, row, keep = _call(
        lambda *refs: _step(n_rows, n_cols, *refs),
        [FIELD, FIELD, FIELD, FIELD, BARE_MARGIN, BARE_MARGIN, ROW, ROW],
        [power, s0, got_n, got_s, got_w, got_e, al, y0, y0_rows, y0_cols, cond, c_rows, c_cols,
         weights, e0, gath, cond_table, tier_table, den, fwd, inv],
        smem=(16, 17),
        scratch=(ENDS, FIELD, ENDS, FIELD),
    )

    got_n, got_s = _exchange(send_n, send_s, "rows")
    (al,) = _call(_align_last, [FIELD], [w1, cond_table, tier_table, den, mat], smem=(1, 2))
    send_w, send_e, pay = _call(_pack, [BARE_SIDE, BARE_SIDE, pay_shape], [w1, got_n, got_s, row])
    got_w, got_e = _exchange(send_w, send_e, "cols")
    gath = _everywhere(pay)
    return tuple(
        _call(
            _finish,
            [FIELD, FIELD, FIELD],
            [s0, y0, y1, r1, z1, w1, got_n, got_s, got_w, got_e, al, weights, keep, gath,
             cond_table, tier_table, den, fwd, inv],
            smem=(14, 15),
        )
    )


def solution(mesh):
    in_specs = (P(None, None, "rows", "cols"), P(None, "rows", "cols"), P(), P(), P(), P())
    out_specs = (P(None, None, "rows", "cols"),) * 3
    return jax.shard_map(shards, mesh=mesh, in_specs=in_specs, out_specs=out_specs, check_vma=False)
```
